256 devices in a mesh: rows: 32 (over y, z), tensor: 8 (over x, core).
Axes of the slice: x: 4, y: 4, z: 8, core: 2. Of those that a mesh axis runs over, the one named last changes fastest.
Arguments:
- token_ids: int32 [256, 4], replicated, may hold values from 0 to 65535
- cache_lengths: int32 [256], P('rows'), may hold values from 160 to 1280, as said below
- doc_ids: int32 [256], replicated, may hold values from 0 to 31
- embed_table: bfloat16 [65536, 8192], P('tensor', 'rows'), may hold values from -10.5 to 10.5
- cache_keys: bfloat16 [256, 1280, 1024], P('rows', None, 'tensor'), may hold values from -700 to 700
- cache_values: bfloat16 [256, 1280, 1024], P('rows', None, 'tensor'), may hold values from -6 to 6
- decode_gain: float32 [8192], P('rows'), may hold values from 0.1 to 1.9
- decode_query: bfloat16 [8192, 8192], P('rows', 'tensor'), may hold values from -0.0625 to 0.0625
- decode_key: bfloat16 [8192, 1024], P('rows', 'tensor'), may hold values from -0.0625 to 0.0625
- decode_value: bfloat16 [8192, 1024], P('rows', 'tensor'), may hold values from -0.0625 to 0.0625
- decode_out: bfloat16 [8192, 8192], P('tensor', 'rows'), may hold values from -0.0625 to 0.0625
- reduce_gain: float32 [8192], P('rows'), may hold values from 0.8 to 10
- reduce_query: bfloat16 [8192, 8192], P('rows', 'tensor'), may hold values from -0.0625 to 0.0625
- reduce_key: bfloat16 [8192, 1024], P('rows', 'tensor'), may hold values from -0.0625 to 0.0625
- reduce_value: bfloat16 [8192, 1024], P('rows', 'tensor'), may hold values from -0.0625 to 0.0625
- reduce_out: bfloat16 [8192, 8192], P('tensor', 'rows'), may hold values from -0.0625 to 0.0625
Outputs:
- reduced: bfloat16 [1024, 8192], P(None, 'rows')
The draws below stay inside these ranges and needn't reach their ends.
Inputs may be any that keep to these rules, and one draw needn't show every extreme that they name: Passage row c holds cache entries at positions below cache_lengths[c]; one row in every draw has a full cache of 1280.
All inputs are finite; a program needn't handle non-finite values.
Results may differ from the reference program's by a relative error of at most 0.035.
The reference program's roundings to bfloat16 on the way count: a program that leaves them out, or rounds other values in their place, can miss the bound.
Values may be sent and summed in bfloat16 or wider, within the bound.
A program may use at most 64 MiB of HBM per device.

```python
import math
import jax
import jax.numpy as jnp
import numpy as np
from jax import lax

D = 8192
HEADS = 64
KV_HEADS = 8
HEAD_DIM = 128
VOCAB = 65536
STEPS = 4
CACHE = 1280
ROWS_ALL = 256
TOKENS = 1024
DOCS = 32


def draw_embed_table(key, part):
    first_key = jax.random.fold_in(key, 0)
    column = jnp.arange(D, dtype=jnp.float32)
    rising = 0.5 * 3.0 ** (column / D)
    values = jnp.clip(jax.random.normal(first_key, (VOCAB, D), jnp.float32), -6.0, 6.0)
    return (values * rising[None, :]).astype(jnp.bfloat16)


def draw_cache_keys(key, part):
    first_key = jax.random.fold_in(key, 0)
    full_shape = (ROWS_ALL, CACHE, KV_HEADS * HEAD_DIM)
    values = jnp.clip(jax.random.normal(first_key, full_shape, jnp.float32), -6.0, 6.0)
    return values.astype(jnp.bfloat16)


def draw_cache_lengths(key, part):
    first_key, second_key, third_key, fourth_key = jax.random.split(key, 4)
    short_len = jax.random.randint(first_key, (ROWS_ALL,), CACHE // 8, CACHE // 4 + 1)
    long_len = jax.random.randint(second_key, (ROWS_ALL,), CACHE // 2, CACHE + 1)
    selector = jax.random.randint(third_key, (ROWS_ALL,), 0, 4)
    lengths = jnp.where(selector == 0, long_len, short_len)
    top_row = jax.random.randint(fourth_key, (), 0, ROWS_ALL)
    return jnp.where(jnp.arange(ROWS_ALL) == top_row, CACHE, lengths).astype(jnp.int32)


def draw_reduce_gain(key, part):
    values = jax.random.uniform(key, (D,), jnp.float32, 0.82, 1.18)
    return values


def plant(drawn, stream_key, least, largest):
    longest = drawn.shape.index(max(drawn.shape))
    spots = []
    for shift in (0, 1):
        where = [jax.random.randint(jax.random.fold_in(stream_key, axis), (), 0, length) for axis, length in enumerate(drawn.shape)]
        where[longest] = (where[longest] + shift) % drawn.shape[longest]
        spots.append(tuple(where))
    return drawn.at[spots[0]].set(least).at[spots[1]].set(largest)


def block_levels(rng, dims, pieces, least, largest):
    gain, own = 1.0, jax.random.fold_in(rng, 6)
    for dim, parts in pieces:
        heights = jnp.exp(jax.random.uniform(jax.random.fold_in(own, dim), (parts,), jnp.float32, least / len(pieces), largest / len(pieces)))
        gain = gain * jnp.repeat(heights, dims[dim] // parts).reshape([-1 if axis == dim else 1 for axis in range(len(dims))])
    return gain


def cumulative_ranks(number_of, slope):
    portions = [(1 << 20) // math.isqrt(grade ** slope) + 1 for grade in range(1, number_of + 1)]
    spread = 1 + sum(portions) // (1 << 30)
    return np.cumsum(np.array([max(1, weight // spread) for weight in portions]))


def skewed_ids(rng, extent, number_of, slope):
    grid = cumulative_ranks(number_of, slope)
    pick = jax.random.randint(jax.random.fold_in(rng, 1), extent, 0, int(grid[number_of - 1]))
    standing = jnp.searchsorted(jnp.asarray(grid, jnp.int32), pick, side="right")
    return jax.random.permutation(jax.random.fold_in(rng, 2), number_of)[standing].astype(jnp.int32)


def noise(key, extent, scale, most, cuts=(), kind=jnp.bfloat16):
    level = block_levels(key, extent, cuts, -0.22, 0.18) if cuts else 1.0
    drawn = jax.random.normal(key, extent, jnp.float32) * scale * level
    return jnp.minimum(jnp.maximum(drawn, -most), most).astype(kind)


def setup_inputs(seed: int = 0) -> dict:
    key_of = jax.random.split(jax.random.key(seed), 17)
    return {
        "token_ids": plant(skewed_ids(key_of[0], (ROWS_ALL, STEPS), VOCAB, 2), jax.random.fold_in(key_of[0], 3), 0, VOCAB - 1).astype(jnp.int32),
        "cache_lengths": draw_cache_lengths(jax.random.fold_in(key_of[16], 71), 0),
        "doc_ids": plant(jax.random.randint(key_of[2], (ROWS_ALL,), 0, DOCS), jax.random.fold_in(key_of[2], 1), 0, DOCS - 1).astype(jnp.int32),
        "embed_table": draw_embed_table(jax.random.fold_in(key_of[16], 71), 0),
        "cache_keys": draw_cache_keys(jax.random.fold_in(key_of[16], 71), 0),
        "cache_values": noise(key_of[5], (ROWS_ALL, CACHE, KV_HEADS * HEAD_DIM), 1.0, 6.0, ((0, 32), (2, 8))),
        "decode_gain": jnp.clip(1.0 + 0.18 * jax.random.normal(key_of[6], (D,), jnp.float32), 0.1, 1.9),
        "decode_query": noise(key_of[7], (D, HEADS * HEAD_DIM), D ** -0.5, 0.0625, ((0, 32), (1, 8))),
        "decode_key": noise(key_of[8], (D, KV_HEADS * HEAD_DIM), D ** -0.5, 0.0625, ((0, 32), (1, 8))),
        "decode_value": noise(key_of[9], (D, KV_HEADS * HEAD_DIM), D ** -0.5, 0.0625, ((0, 32), (1, 8))),
        "decode_out": noise(key_of[10], (HEADS * HEAD_DIM, D), (HEADS * HEAD_DIM) ** -0.5, 0.0625, ((0, 8), (1, 32))),
        "reduce_gain": draw_reduce_gain(jax.random.fold_in(key_of[16], 71), 0),
        "reduce_query": noise(key_of[12], (D, HEADS * HEAD_DIM), D ** -0.5, 0.0625, ((0, 32), (1, 8))),
        "reduce_key": noise(key_of[13], (D, KV_HEADS * HEAD_DIM), D ** -0.5, 0.0625, ((0, 32), (1, 8))),
        "reduce_value": noise(key_of[14], (D, KV_HEADS * HEAD_DIM), D ** -0.5, 0.0625, ((0, 32), (1, 8))),
        "reduce_out": noise(key_of[15], (HEADS * HEAD_DIM, D), (HEADS * HEAD_DIM) ** -0.5, 0.0625, ((0, 8), (1, 32))),
    }


EPSILON = 1e-05
ROPE_BASE = 500000.0

def rotate(vectors, positions):
    half_dim = vectors.shape[-1] // 2
    frequencies = ROPE_BASE ** (-2.0 * jnp.arange(half_dim, dtype=jnp.float32) / vectors.shape[-1])
    angles = positions.astype(jnp.float32)[..., None] * frequencies
    cosine = jnp.cos(angles)
    sine_part = jnp.sin(angles)
    lower_half = vectors[..., :half_dim]
    upper_half = vectors[..., half_dim:]
    return jnp.concatenate([lower_half * cosine - upper_half * sine_part, upper_half * cosine + lower_half * sine_part], axis=-1)

def soft_weights(scores):
    weights = jax.nn.softmax(scores, axis=-1).astype(jnp.bfloat16)
    weights = lax.optimization_barrier(weights)
    return weights.astype(jnp.float32)

def attend_row(inputs):
    query_row, keys_new, values_new, keys_old, values_old, length = inputs
    group_size = HEADS // KV_HEADS
    query_row = query_row.reshape(STEPS, KV_HEADS, group_size, HEAD_DIM).astype(jnp.float32)
    keys_all = jnp.concatenate([keys_old.reshape(CACHE, KV_HEADS, HEAD_DIM).astype(jnp.float32), keys_new.astype(jnp.float32)], axis=0)
    values_all = jnp.concatenate([values_old.reshape(CACHE, KV_HEADS, HEAD_DIM).astype(jnp.float32), values_new.astype(jnp.float32)], axis=0)
    scores = jnp.einsum('skgd,ckd->skgc', query_row, keys_all) * HEAD_DIM ** (-0.5)
    slot_ids = jnp.arange(CACHE + STEPS, dtype=jnp.int32)
    step_ids = jnp.arange(STEPS, dtype=jnp.int32)
    allowed = jnp.where(slot_ids[None, :] < CACHE, slot_ids[None, :] < length, slot_ids[None, :] - CACHE <= step_ids[:, None])
    scores = jnp.where(allowed[:, None, None, :], scores, -jnp.inf)
    weights = soft_weights(scores)
    output = jnp.einsum('skgc,ckd->skgd', weights, values_all)
    return output.reshape(STEPS, HEADS * HEAD_DIM).astype(jnp.bfloat16)

def reference(token_ids, cache_lengths, doc_ids, embed_table, cache_keys, cache_values, decode_gain, decode_query, decode_key, decode_value, decode_out, reduce_gain, reduce_query, reduce_key, reduce_value, reduce_out):
    group_size = HEADS // KV_HEADS
    step_ids = jnp.arange(STEPS, dtype=jnp.int32)
    flat_ids = token_ids.reshape(TOKENS)
    embedded = jnp.take(embed_table, flat_ids, axis=0).astype(jnp.float32)
    decode_scale = lax.rsqrt(lax.optimization_barrier(jnp.mean(embedded * embedded, axis=1)) + EPSILON)
    decode_normed = (embedded * decode_gain[None, :]).astype(jnp.bfloat16)
    decode_q = decode_scale[:, None] * jnp.dot(decode_normed, decode_query, preferred_element_type=jnp.float32)
    decode_k = decode_scale[:, None] * jnp.dot(decode_normed, decode_key, preferred_element_type=jnp.float32)
    decode_v = decode_scale[:, None] * jnp.dot(decode_normed, decode_value, preferred_element_type=jnp.float32)
    new_positions = (cache_lengths[:, None] + step_ids[None, :]).reshape(TOKENS, 1)
    decode_queries = rotate(decode_q.reshape(TOKENS, HEADS, HEAD_DIM), new_positions).astype(jnp.bfloat16)
    new_keys = rotate(decode_k.reshape(TOKENS, KV_HEADS, HEAD_DIM), new_positions).astype(jnp.bfloat16)
    new_values = decode_v.astype(jnp.bfloat16)
    attended = lax.map(attend_row, (decode_queries.reshape(ROWS_ALL, STEPS, HEADS, HEAD_DIM), new_keys.reshape(ROWS_ALL, STEPS, KV_HEADS, HEAD_DIM), new_values.reshape(ROWS_ALL, STEPS, KV_HEADS, HEAD_DIM), cache_keys, cache_values, cache_lengths))
    attended = attended.reshape(TOKENS, HEADS * HEAD_DIM)
    summary = (embedded + jnp.dot(attended, decode_out, preferred_element_type=jnp.float32)).astype(jnp.bfloat16)
    summary_wide = summary.astype(jnp.float32)
    reduce_scale = lax.rsqrt(lax.optimization_barrier(jnp.mean(summary_wide * summary_wide, axis=1)) + EPSILON)
    reduce_normed = (summary_wide * reduce_gain[None, :]).astype(jnp.bfloat16)
    reduce_q = reduce_scale[:, None] * jnp.dot(reduce_normed, reduce_query, preferred_element_type=jnp.float32)
    reduce_k = reduce_scale[:, None] * jnp.dot(reduce_normed, reduce_key, preferred_element_type=jnp.float32)
    reduce_v = reduce_scale[:, None] * jnp.dot(reduce_normed, reduce_value, preferred_element_type=jnp.float32)
    passage_index = jnp.arange(ROWS_ALL, dtype=jnp.int32)
    earlier = lax.optimization_barrier(jnp.sum(((doc_ids[None, :] == doc_ids[:, None]) & (passage_index[None, :] < passage_index[:, None])).astype(jnp.int32), axis=1))
    doc_positions = (earlier[:, None] * STEPS + step_ids[None, :]).reshape(TOKENS, 1)
    doc_tokens = (doc_ids[:, None] + jnp.zeros((1, STEPS), jnp.int32)).reshape(TOKENS)
    reduce_queries = rotate(reduce_q.reshape(TOKENS, HEADS, HEAD_DIM), doc_positions).astype(jnp.bfloat16)
    reduce_keys = rotate(reduce_k.reshape(TOKENS, KV_HEADS, HEAD_DIM), doc_positions).astype(jnp.bfloat16)
    reduce_values = reduce_v.astype(jnp.bfloat16).reshape(TOKENS, KV_HEADS, HEAD_DIM)
    token_index = jnp.arange(TOKENS, dtype=jnp.int32)
    allowed = (doc_tokens[:, None] == doc_tokens[None, :]) & (token_index[None, :] <= token_index[:, None])
    head_queries = reduce_queries.reshape(TOKENS, KV_HEADS, group_size, HEAD_DIM).transpose(1, 0, 2, 3)
    head_keys = reduce_keys.transpose(1, 0, 2)
    head_values = reduce_values.transpose(1, 0, 2)

    def attend_head(inputs):
        query_head, key_head, value_head = inputs
        scores = jnp.einsum('tgd,ud->tgu', query_head.astype(jnp.float32), key_head.astype(jnp.float32)) * HEAD_DIM ** (-0.5)
        scores = jnp.where(allowed[:, None, :], scores, -jnp.inf)
        weights = soft_weights(scores)
        return jnp.einsum('tgu,ud->tgd', weights, value_head.astype(jnp.float32)).astype(jnp.bfloat16)
    reduce_attended = lax.map(attend_head, (head_queries, head_keys, head_values))
    reduce_attended = reduce_attended.transpose(1, 0, 2, 3).reshape(TOKENS, HEADS * HEAD_DIM)
    return (summary_wide + jnp.dot(reduce_attended, reduce_out, preferred_element_type=jnp.float32)).astype(jnp.bfloat16)
```

```python
import jax
import jax.numpy as jnp
from jax import lax
from jax.sharding import PartitionSpec as P

D = 8192
HEAD_DIM = 128


EPSILON = 1e-05
ROPE_BASE = 500000.0


def rotate(vectors, positions):
    half_dim = vectors.shape[-1] // 2
    frequencies = ROPE_BASE ** (-2.0 * jnp.arange(half_dim, dtype=jnp.float32) / vectors.shape[-1])
    angles = positions.astype(jnp.float32)[..., None] * frequencies
    cosine = jnp.cos(angles)
    sine_part = jnp.sin(angles)
    lower_half = vectors[..., :half_dim]
    upper_half = vectors[..., half_dim:]
    return jnp.concatenate(
        [
            lower_half * cosine - upper_half * sine_part,
            upper_half * cosine + lower_half * sine_part,
        ],
        axis=-1,
    )


def width_total(partial_value):
    return lax.psum(partial_value, "tensor")


def row_scale(summed):
    return lax.rsqrt(summed / D + EPSILON)


def head_terms(normed, matrices, squares, groups):
    partial = jnp.concatenate(
        [jnp.dot(normed, matrix, preferred_element_type=jnp.float32) for matrix in matrices],
        axis=1,
    )
    tokens, cols = partial.shape
    own = tokens // groups
    payload = jnp.concatenate(
        [partial.reshape(groups, own * cols), squares.reshape(groups, own)], axis=1
    ).reshape(groups, 8, (own * cols + own) // 8)
    summed = lax.psum_scatter(payload, "rows", scatter_dimension=0, tiled=True)
    summed = summed.reshape(own * cols + own)
    return summed[: own * cols].reshape(own, cols), summed[own * cols :]


def head_mix(attended, matrix):
    return jnp.dot(
        lax.all_gather(attended, "rows", axis=0, tiled=True),
        matrix,
        preferred_element_type=jnp.float32,
    )


def per_device(
    token_ids,
    cache_lengths,
    doc_ids,
    embed_table,
    cache_keys,
    cache_values,
    decode_gain,
    decode_query,
    decode_key,
    decode_value,
    decode_out,
    reduce_gain,
    reduce_query,
    reduce_key,
    reduce_value,
    reduce_out,
):
    step_count = token_ids.shape[1]
    passage_count = token_ids.shape[0]
    token_count = passage_count * step_count
    own_passages = cache_lengths.shape[0]
    own_tokens = own_passages * step_count
    row_first = lax.axis_index("rows") * own_tokens
    query_cols = decode_query.shape[1]
    kv_cols = decode_key.shape[1]
    local_heads = query_cols // HEAD_DIM
    local_kv = kv_cols // HEAD_DIM
    group_size = local_heads // local_kv
    score_scale = HEAD_DIM ** (-0.5)
    step_ids = jnp.arange(step_count, dtype=jnp.int32)
    vocab_part = embed_table.shape[0]
    local_ids = token_ids.reshape(token_count) - lax.axis_index("tensor") * vocab_part
    inside = (local_ids >= 0) & (local_ids < vocab_part)
    picked = jnp.take(embed_table, jnp.clip(local_ids, 0, vocab_part - 1), axis=0)
    picked = jnp.where(inside[:, None], picked, jnp.zeros_like(picked))
    embedded = width_total(picked).astype(jnp.float32)
    row_groups = token_count // own_tokens
    normed = (embedded * decode_gain[None, :]).astype(jnp.bfloat16)
    projected, dec_squares = head_terms(
        normed,
        (decode_query, decode_key, decode_value),
        jnp.sum(embedded * embedded, axis=1),
        row_groups,
    )
    projected = projected * row_scale(dec_squares)[:, None]
    positions = (cache_lengths[:, None] + step_ids[None, :]).reshape(own_tokens, 1)
    queries = rotate(
        projected[:, :query_cols].reshape(own_tokens, local_heads, HEAD_DIM), positions
    ).astype(jnp.bfloat16)
    keys_new = rotate(
        projected[:, query_cols : query_cols + kv_cols].reshape(own_tokens, local_kv, HEAD_DIM),
        positions,
    ).astype(jnp.bfloat16)
    values_new = projected[:, query_cols + kv_cols :].astype(jnp.bfloat16)
    queries = queries.reshape(own_passages, step_count, local_kv, group_size, HEAD_DIM)
    keys_new = keys_new.reshape(own_passages, step_count, local_kv, HEAD_DIM)
    values_new = values_new.reshape(own_passages, step_count, local_kv, HEAD_DIM)
    capacity = cache_keys.shape[1]
    keys_old = cache_keys.reshape(own_passages, capacity, local_kv, HEAD_DIM)
    values_old = cache_values.reshape(own_passages, capacity, local_kv, HEAD_DIM)
    new_scores = (
        jnp.einsum("rskgd,rtkd->rskgt", queries, keys_new, preferred_element_type=jnp.float32)
        * score_scale
    )
    causal = step_ids[None, :] <= step_ids[:, None]
    new_scores = jnp.where(causal[None, :, None, None, :], new_scores, -jnp.inf)
    old_scores = (
        jnp.einsum("rskgd,rckd->rskgc", queries, keys_old, preferred_element_type=jnp.float32)
        * score_scale
    )
    slot_ids = jnp.arange(capacity, dtype=jnp.int32)
    live_mask = slot_ids[None, :] < cache_lengths[:, None]
    old_scores = jnp.where(live_mask[:, None, None, None, :], old_scores, -jnp.inf)
    highest = jnp.maximum(jnp.max(old_scores, axis=-1), jnp.max(new_scores, axis=-1))
    old_exp = jnp.exp(old_scores - highest[..., None])
    new_exp = jnp.exp(new_scores - highest[..., None])
    summed = jnp.sum(old_exp, axis=-1) + jnp.sum(new_exp, axis=-1)
    old_weights = (old_exp / summed[..., None]).astype(jnp.bfloat16)
    new_weights = (new_exp / summed[..., None]).astype(jnp.bfloat16)
    attended = jnp.einsum(
        "rskgc,rckd->rskgd", old_weights, values_old, preferred_element_type=jnp.float32
    )
    attended = attended + jnp.einsum(
        "rskgt,rtkd->rskgd", new_weights, values_new, preferred_element_type=jnp.float32
    )
    attended = attended.reshape(own_tokens, query_cols).astype(jnp.bfloat16)
    partial_value = head_mix(attended, decode_out)
    summary = (embedded + width_total(partial_value)).astype(jnp.bfloat16)
    summary_wide = summary.astype(jnp.float32)
    normed_red = (summary_wide * reduce_gain[None, :]).astype(jnp.bfloat16)
    passage_index = jnp.arange(passage_count, dtype=jnp.int32)
    earlier = jnp.sum(
        (
            (doc_ids[None, :] == doc_ids[:, None])
            & (passage_index[None, :] < passage_index[:, None])
        ).astype(jnp.int32),
        axis=1,
    )
    doc_positions = (earlier[:, None] * step_count + step_ids[None, :]).reshape(token_count, 1)
    doc_tokens = (doc_ids[:, None] + jnp.zeros_like(step_ids)[None, :]).reshape(token_count)
    own_positions = lax.dynamic_slice_in_dim(doc_positions, row_first, own_tokens, 0)
    projected, red_squares = head_terms(
        normed_red,
        (reduce_query, reduce_key, reduce_value),
        jnp.sum(summary_wide * summary_wide, axis=1),
        row_groups,
    )
    projected = projected * row_scale(red_squares)[:, None]
    queries_red = rotate(
        projected[:, :query_cols].reshape(own_tokens, local_heads, HEAD_DIM), own_positions
    ).astype(jnp.bfloat16)
    keys_own = (
        rotate(
            projected[:, query_cols : query_cols + kv_cols].reshape(own_tokens, local_kv, HEAD_DIM),
            own_positions,
        )
        .astype(jnp.bfloat16)
        .reshape(own_tokens, kv_cols)
    )
    values_own = projected[:, query_cols + kv_cols :].astype(jnp.bfloat16)
    kv_red = lax.all_gather(
        jnp.concatenate([keys_own, values_own], axis=1), "rows", axis=0, tiled=True
    )
    keys_red, values_red = kv_red[:, :kv_cols], kv_red[:, kv_cols:]
    queries_red = queries_red.reshape(own_tokens, local_kv, group_size, HEAD_DIM)
    keys_red = keys_red.reshape(token_count, local_kv, HEAD_DIM)
    values_red = values_red.reshape(token_count, local_kv, HEAD_DIM)
    token_index = jnp.arange(token_count, dtype=jnp.int32)
    own_index = row_first + jnp.arange(own_tokens, dtype=jnp.int32)
    own_docs = lax.dynamic_slice_in_dim(doc_tokens, row_first, own_tokens, 0)
    allowed = (own_docs[:, None] == doc_tokens[None, :]) & (
        token_index[None, :] <= own_index[:, None]
    )
    red_scores = (
        jnp.einsum("tkgd,ukd->tkgu", queries_red, keys_red, preferred_element_type=jnp.float32)
        * score_scale
    )
    red_scores = jnp.where(allowed[:, None, None, :], red_scores, -jnp.inf)
    red_high = jnp.max(red_scores, axis=-1)
    red_exp = jnp.exp(red_scores - red_high[..., None])
    red_weights = (red_exp / jnp.sum(red_exp, axis=-1)[..., None]).astype(jnp.bfloat16)
    red_out = jnp.einsum(
        "tkgu,ukd->tkgd", red_weights, values_red, preferred_element_type=jnp.float32
    )
    red_out = red_out.reshape(own_tokens, query_cols).astype(jnp.bfloat16)
    return (summary_wide + width_total(head_mix(red_out, reduce_out))).astype(jnp.bfloat16)


def solution(mesh):
    return jax.shard_map(
        per_device,
        mesh=mesh,
        in_specs=(
            P(),
            P("rows"),
            P(),
            P("tensor", "rows"),
            P("rows", None, "tensor"),
            P("rows", None, "tensor"),
            P("rows"),
            P("rows", "tensor"),
            P("rows", "tensor"),
            P("rows", "tensor"),
            P("tensor", "rows"),
            P("rows"),
            P("rows", "tensor"),
            P("rows", "tensor"),
            P("rows", "tensor"),
            P("tensor", "rows"),
        ),
        out_specs=P(None, "rows"),
        check_vma=False,
    )
```
